32 devices in a mesh: row: 4 (over y, core), col: 8 (over z, x).
Axes of the slice: x: 2, y: 2, z: 4, core: 2. Of those that a mesh axis runs over, the one named last changes fastest.
Arguments:
- left: bfloat16 [128, 8192], P('col', 'row'), may hold values from -6 to 6
- right: bfloat16 [128, 8192], P('row', 'col'), may hold values from -6 to 6
- proj: bfloat16 [1024, 128], replicated, may hold values from -2 to 2
- bias: float32 [128], replicated, may hold values from -1 to 1
- pair_grad: bfloat16 [256, 256, 128], P('row', 'col'), may hold values from -0.1875 to 0.1875
Outputs:
- pair_out: bfloat16 [256, 256, 128], P('row', 'col')
- left_grad: float32 [128, 8192], P('col', 'row')
- right_grad: float32 [128, 8192], P('row', 'col')
- proj_grad: float32 [1024, 128], replicated
The draws below stay inside these ranges and needn't reach their ends.
All inputs are finite; a program needn't handle non-finite values.
Results may differ from the reference program's by a relative error of at most 0.0056.
Values may be sent and summed in bfloat16 or wider, within the bound.
A program may use at most 128 MiB of HBM per device.

```python
import jax
import jax.numpy as jnp
from jax import lax

CH = 32
PAIR = 128
SEQS = 128
TOK_DEV = 64
OUTER = 1024
TOKENS = 256


def shard_levels(rng, dims, cuts, smallest, high):
    factor_of = 1.0
    for axis_at, parts in cuts:
        steps = jax.random.uniform(jax.random.fold_in(jax.random.fold_in(rng, 6), axis_at), (parts,), jnp.float32, smallest / len(cuts), high / len(cuts))
        factor_of = factor_of * jnp.repeat(jnp.exp(steps), dims[axis_at] // parts).reshape((-1,) + (1,) * (len(dims) - 1 - axis_at))
    return factor_of


def gaussian(stream_key, dims, deviation, limit, cuts=(), held_as=jnp.bfloat16):
    array = deviation * jax.random.normal(stream_key, dims, jnp.float32)
    if cuts:
        array = array * shard_levels(stream_key, dims, cuts, -0.22, 0.18)
    return jnp.clip(array, -limit, limit).astype(held_as)


def setup_inputs(seed: int = 0) -> dict:
    key_of = jax.random.split(jax.random.key(seed), 6)
    left = gaussian(key_of[0], (SEQS, TOKENS * CH), 1.0, 6.0, ((0, 8), (1, 4)))
    right = gaussian(key_of[1], (SEQS, TOKENS * CH), 1.0, 6.0, ((0, 4), (1, 8)))
    proj = gaussian(key_of[2], (OUTER, PAIR), (OUTER // SEQS) ** -0.5, 2.0)
    bias = jnp.clip(jax.random.uniform(key_of[3], (PAIR,), jnp.float32, -1.0, 1.0), -1.0, 1.0)
    pair_grad = gaussian(key_of[4], (TOKENS, TOKENS, PAIR), 0.03, 0.1875, ((0, 4), (1, 8)))
    return {"left": left, "right": right, "proj": proj, "bias": bias, "pair_grad": pair_grad}


def reference(left, right, proj, bias, pair_grad):
    left_cube = left.reshape(SEQS, TOKENS, CH)
    right_cube = right.reshape(SEQS, TOKENS, CH)
    right_wide = right_cube.astype(jnp.float32)
    blocks = TOKENS // TOK_DEV

    def step_block(totals, index_block):
        weight_total, right_total = totals
        first_row = (index_block * TOK_DEV).astype(jnp.int32)
        left_block = lax.dynamic_slice_in_dim(left_cube, first_row, TOK_DEV, 1)
        grad_block = lax.dynamic_slice_in_dim(pair_grad, first_row, TOK_DEV, 0)
        outers = jnp.einsum('sic,sje->ijce', left_block.astype(jnp.float32), right_wide) / SEQS
        outers = outers.astype(jnp.bfloat16).reshape(TOK_DEV * TOKENS, OUTER)
        preact = jnp.dot(outers, proj, preferred_element_type=jnp.float32) + bias
        active = jnp.maximum(preact, 0.0)
        pair_block = (active * active).astype(jnp.bfloat16).reshape(TOK_DEV, TOKENS, PAIR)
        grad_pre = (grad_block.reshape(TOK_DEV * TOKENS, PAIR).astype(jnp.float32) * 2.0 * active).astype(jnp.bfloat16)
        weight_total = weight_total + jnp.dot(outers.T, grad_pre, preferred_element_type=jnp.float32)
        grad_outer = jnp.dot(grad_pre, proj.T, preferred_element_type=jnp.float32).astype(jnp.bfloat16)
        grad_outer = grad_outer.reshape(TOK_DEV, TOKENS, CH, CH).astype(jnp.float32)
        left_block_grad = jnp.einsum('ijce,sje->sic', grad_outer, right_wide) / SEQS
        right_total = right_total + jnp.einsum('ijce,sic->sje', grad_outer, left_block.astype(jnp.float32)) / SEQS
        return (weight_total, right_total), (pair_block, left_block_grad)

    start = (jnp.zeros((OUTER, PAIR), jnp.float32), jnp.zeros((SEQS, TOKENS, CH), jnp.float32))
    (proj_grad, right_total), (pair_blocks, left_blocks) = lax.scan(step_block, start, jnp.arange(blocks, dtype=jnp.int32))
    pair_out = pair_blocks.reshape(TOKENS, TOKENS, PAIR)
    left_grad = jnp.transpose(left_blocks, (1, 0, 2, 3)).reshape(SEQS, TOKENS * CH)
    right_grad = right_total.reshape(SEQS, TOKENS * CH)
    return pair_out, left_grad, right_grad, proj_grad
```

```python
import functools

import jax
import jax.numpy as jnp
from jax import lax
from jax.experimental import pallas as pl
from jax.experimental.pallas import tpu as pltpu
from jax.sharding import PartitionSpec as P

CH = 32
PAIR = 128
LANES = 128
PACK = LANES // CH
TILE = 256
LONG = 512
PARTS = 2
MESH = pl.DeviceIdType.MESH
F32 = jnp.float32
BF16 = jnp.bfloat16


def inner_size(n):
    inner = 1
    while inner * inner * 4 <= n and n % (inner * 2) == 0:
        inner *= 2
    return inner


def dot(a, b):
    return jnp.dot(a, b, preferred_element_type=F32)


def dot_t(a, b):
    return lax.dot_general(a, b, (((1,), (1,)), ((), ())), preferred_element_type=F32)


def aligned(index, size):
    return pl.ds(pl.multiple_of(index * size, size), size)


def fold(tiles, low, width):
    if len(tiles) == 1:
        return tiles[0][0]
    same = jnp.where(low, tiles[0][0], tiles[1][1])
    crossed = jnp.where(low, tiles[1][0], tiles[0][1])
    return same + pltpu.roll(crossed, width, 1)


def kernel(
    R, C, share,
    left, right, proj, bias, pair_grad,
    pair_out, left_out, right_out, proj_out,
    lbuf, rbuf, ltrans, bt, rtrans, r2, r2t, projt, pairs_f, pgt, sq, outer, gpre, gouter, lperm,
    pterm, psend, precv, psum, pshare, pparts, pgather,
    rtmp, rown, rsend, rparts, lown, lsend, lxparts, lzsend, lzparts,
    s_lz, r_lz, s_lx, r_lx, s_rg, r_rg,
    s_pc, r_pc, s_ps, r_ps, s_pa, r_pa, s_pe, r_pe,
    s_rs, r_rs, s_lsx, r_lsx, s_lsz, r_lsz,
):
    C2 = inner_size(C)
    C1 = C // C2
    row, col = lax.axis_index("row"), lax.axis_index("col")
    z, x = col // C2, lax.rem(col, C2)
    lseq, lwide = left.shape
    seqs = lseq * C
    rwide = right.shape[1]
    I, J = lwide // CH, rwide // CH
    JL = LANES // I
    JH = J // JL
    pairs = I * J
    scale = 1.0 / seqs

    def send(src, dst, ssem, rsem, to_row, to_col):
        return pltpu.make_async_remote_copy(
            src_ref=src, dst_ref=dst, send_sem=ssem, recv_sem=rsem,
            device_id=(to_row, to_col), device_id_type=MESH,
        )

    def zpeer(d):
        return lax.rem(z + d, C1)

    def xpeer(d):
        return lax.rem(x + d, C2)

    def rpeer(d):
        return lax.rem(row + d, R)

    barrier = pltpu.get_barrier_semaphore()
    for d in range(1, R):
        pl.semaphore_signal(barrier, inc=1, device_id=(rpeer(d), col), device_id_type=MESH)
    for d in range(1, C2):
        pl.semaphore_signal(
            barrier, inc=1, device_id=(row, z * C2 + xpeer(d)), device_id_type=MESH)
    for d in range(1, C1):
        pl.semaphore_signal(
            barrier, inc=1, device_id=(row, zpeer(d) * C2 + x), device_id_type=MESH)
    pl.semaphore_wait(barrier, R - 1 + C1 - 1 + C2 - 1)

    pending = []

    def go(copy):
        copy.start()
        pending.append(copy)
        return copy

    lchunk = lwide // PARTS
    for p in range(PARTS):
        piece = left.at[:, p * lchunk:(p + 1) * lchunk]
        for d in range(1, C1):
            go(send(
                piece, lbuf.at[p, col], s_lz.at[p, d - 1], r_lz.at[p, d - 1],
                row, zpeer(d) * C2 + x))
        for d in range(1, C2):
            go(send(
                piece, lbuf.at[p, col], s_lx.at[p, d - 1, 0], r_lx.at[p, d - 1, 0],
                row, z * C2 + xpeer(d)))
        if p == 0:
            for d in range(1, R):
                go(send(right, rbuf.at[row], s_rg.at[d - 1], r_rg.at[d - 1], rpeer(d), col))

    for p in range(PARTS):
        lbuf[p, col] = left[:, p * lchunk:(p + 1) * lchunk]
    rbuf[row] = right[...]

    bt[...] = jnp.zeros_like(bt)
    projt[...] = proj[...].astype(F32).T.astype(BF16)
    pairs_f[...] = pair_grad[...].astype(F32).reshape(pairs, PAIR)
    bias_t = jnp.broadcast_to(bias[...], (LANES, PAIR)).T

    @pl.loop(0, JH, unroll=True)
    def _(h):
        block = jnp.concatenate(
            [pairs_f[pl.ds(h * JL + a, I, stride=J), :] for a in range(JL)], axis=0)
        pgt[:, aligned(h, LANES)] = block.T

    def pass_on(p):
        for d in range(1, C1):
            block = lax.rem(z + C1 - d, C1) * C2 + x
            send(
                lbuf.at[p, block], lbuf.at[p, block], s_lz.at[p, d - 1], r_lz.at[p, d - 1],
                row, col).wait_recv()
            for k in range(1, C2):
                go(send(
                    lbuf.at[p, block], lbuf.at[p, block], s_lx.at[p, k - 1, d],
                    r_lx.at[p, k - 1, d], row, z * C2 + xpeer(k)))

    ipart = I // PARTS

    def arrive(p):
        for d in range(C1):
            for k in range(1, C2):
                block = lax.rem(z + C1 - d, C1) * C2 + lax.rem(x + C2 - k, C2)
                send(
                    lbuf.at[p, block], lbuf.at[p, block], s_lx.at[p, k - 1, d],
                    r_lx.at[p, k - 1, d], row, col).wait_recv()
        ltrans[...] = lbuf[p].astype(F32).reshape(seqs, lchunk).T

        @pl.loop(0, CH, unroll=True)
        def _(c):
            block = ltrans[pl.ds(c, ipart, stride=CH), :].astype(BF16)
            for a in range(JL):
                bt[
                    pl.ds(pl.multiple_of(c * LANES + a * I + p * ipart, ipart), ipart),
                    a * seqs:(a + 1) * seqs
                ] = block

    pass_on(0)
    for d in range(1, R):
        source = lax.rem(row + R - d, R)
        send(right, rbuf.at[source], s_rg.at[d - 1], r_rg.at[d - 1], row, col).wait_recv()

    rtrans[...] = rbuf[...].astype(F32).reshape(seqs, rwide).T * scale
    for h in range(JH):
        for a in range(JL):
            at = (h * JL + a) * CH
            r2[h * CH:(h + 1) * CH, a * seqs:(a + 1) * seqs] = rtrans[at:at + CH, :].astype(BF16)
    r2t[...] = r2[...].astype(F32).T.astype(BF16)

    for p in range(PARTS):
        arrive(p)
        if p + 1 < PARTS:
            pass_on(p + 1)

    per = LONG // LANES

    @pl.loop(0, CH * LANES // LONG, unroll=True)
    def _(t):
        part = dot_t(r2[...], bt[aligned(t, LONG), :]).astype(BF16)
        for k in range(per):
            for h in range(JH):
                outer[aligned(t * per + k, CH), h * LANES:(h + 1) * LANES] = (
                    part[h * CH:(h + 1) * CH, k * LANES:(k + 1) * LANES])

    wide_bias = jnp.concatenate([bias_t] * per, axis=1)

    @pl.loop(0, pairs // LONG, unroll=True)
    def _(t):
        here = aligned(t, LONG)
        active = jnp.maximum(dot(projt[...], outer[:, here]) + wide_bias, 0.0)
        sq[:, here] = active * active
        gpre[:, here] = (pgt[:, here] * 2.0 * active).astype(BF16)

    half = pterm.shape[0] // 2
    core = lax.rem(row, 2)

    def proj_term(at):
        @pl.loop(0, half // TILE, unroll=True)
        def _(t):
            rows = pl.ds(pl.multiple_of(at * half + t * TILE, TILE), TILE)
            pterm[rows, :] = dot_t(outer[rows, :], gpre[...])

    if share:
        other = row + 1 - 2 * core
        count = half // share
        me = (row // 2) * C + col
        proj_term(1 - core)
        psend[...] = pterm[aligned(1 - core, half), :].astype(BF16)
        swap = go(send(psend, precv, s_pc, r_pc, other, col))
        proj_term(core)

        def owner(k):
            return (k // C) * 2 + core, lax.rem(k, C)

        def spread_sum():
            swap.wait_recv()
            both = (pterm[aligned(core, half), :] + precv[...].astype(F32)).reshape(count, share, PAIR)
            psum[...] = both
            pshare[...] = both.astype(BF16)
            scatter = []
            for d in range(1, count):
                k = lax.rem(me + d, count)
                scatter.append(go(send(
                    pshare.at[k], pparts.at[d - 1], s_ps.at[d - 1], r_ps.at[d - 1], *owner(k))))
            return scatter
    else:
        proj_term(0)
        proj_term(1)

    low = lax.broadcasted_iota(jnp.int32, (seqs, LANES), 1) < I
    inner = {}
    for p in range(PARTS):
        cpart = CH // PARTS

        @pl.loop(0, cpart * CH // LANES, unroll=True)
        def _(t):
            part = dot(proj[aligned(p * (cpart * CH // LANES) + t, LANES), :], gpre[...]).astype(BF16)
            for k in range(PACK):
                c = (p * (cpart // PACK) + t) * PACK + k
                for h in range(JH):
                    gouter[h * CH:(h + 1) * CH, aligned(c, LANES)] = (
                        part[k * CH:(k + 1) * CH, h * LANES:(h + 1) * LANES])

        @pl.loop(0, cpart * LANES // LONG, unroll=True)
        def _(t):
            part = dot(r2t[...], gouter[:, aligned(p * (cpart * LANES // LONG) + t, LONG)])
            done = []
            for g in range(LONG // LANES // JL):
                tiles = [
                    [
                        part[b * seqs:(b + 1) * seqs, (g * JL + k) * LANES:(g * JL + k + 1) * LANES]
                        for b in range(JL)
                    ]
                    for k in range(JL)
                ]
                done.append(fold(tiles, low, I))
            total = jnp.concatenate(done, axis=1).reshape(C, lseq, LONG // JL)
            lown[p, :, :, aligned(t, LONG // JL)] = total
            lsend[p, :, :, aligned(t, LONG // JL)] = total.astype(BF16)

        for d in list(range(1, C1)) + [0]:
            for k in range(1, C2):
                inner[p, d, k] = go(send(
                    lsend.at[p, zpeer(d) * C2 + xpeer(k)], lxparts.at[p, k - 1, d],
                    s_lsx.at[p, k - 1, d], r_lsx.at[p, k - 1, d], row, z * C2 + xpeer(k)))

        if p == 0 and share:
            scatter = spread_sum()

    @pl.loop(0, JH * CH // TILE, unroll=True)
    def _(t):
        part = dot(gouter[aligned(t, TILE), :], bt[...]) * scale
        for h in range(TILE // CH):
            for a in range(JL):
                rtmp[aligned((t * (TILE // CH) + h) * JL + a, CH), :] = (
                    part[h * CH:(h + 1) * CH, a * seqs:(a + 1) * seqs])

    turned = rtmp[...].T.reshape(R, seqs // R, rwide)
    rown[...] = turned
    rsend[...] = turned.astype(BF16)
    rights = [
        go(send(rsend.at[rpeer(d)], rparts.at[d - 1], s_rs.at[d - 1], r_rs.at[d - 1], rpeer(d), col))
        for d in range(1, R)
    ]

    @pl.loop(0, JH, unroll=True)
    def _(h):
        block = sq[:, aligned(h, LANES)].T
        for a in range(JL):
            pairs_f[pl.ds(h * JL + a, I, stride=J), :] = block[a * I:(a + 1) * I, :]

    pair_out[...] = pairs_f[...].reshape(I, J, PAIR).astype(BF16)

    outers = {}

    def pass_sums(p):
        for d in range(1, C1):
            total = lown[p, zpeer(d) * C2 + x]
            for k in range(1, C2):
                inner[p, d, k].wait_recv()
                total = total + lxparts[p, k - 1, d].astype(F32)
            lzsend[p, d - 1] = total.astype(BF16)
            outers[p, d] = go(send(
                lzsend.at[p, d - 1], lzparts.at[p, d - 1], s_lsz.at[p, d - 1],
                r_lsz.at[p, d - 1], row, zpeer(d) * C2 + x))

    pass_sums(0)

    if share:
        for copy in scatter:
            copy.wait_recv()
        total = psum[me]
        for d in range(1, count):
            total = total + pparts[d - 1].astype(F32)
        pgather[core, me] = total.astype(BF16)
        for d in range(1, count):
            k = lax.rem(me + d, count)
            go(send(
                pgather.at[core, me], pgather.at[core, me], s_pa.at[d - 1], r_pa.at[d - 1],
                *owner(k)))
    else:
        proj_out[...] = pterm[...]

    for p in range(1, PARTS):
        pass_sums(p)

    for copy in rights:
        copy.wait_recv()
    total = rown[row]
    for d in range(1, R):
        total = total + rparts[d - 1].astype(F32)
    right_out[...] = total

    if share:
        for d in range(1, count):
            k = lax.rem(me + count - d, count)
            send(
                pgather.at[core, me], pgather.at[core, k], s_pa.at[d - 1], r_pa.at[d - 1],
                *owner(k)).wait_recv()
        swap = go(send(pgather.at[core], pgather.at[core], s_pe, r_pe, other, col))

    for p in range(PARTS):
        total = lown[p, col]
        for k in range(1, C2):
            inner[p, 0, k].wait_recv()
            total = total + lxparts[p, k - 1, 0].astype(F32)
        for d in range(1, C1):
            outers[p, d].wait_recv()
            total = total + lzparts[p, d - 1].astype(F32)
        lperm[p * lchunk:(p + 1) * lchunk, :] = total.T
    for g in range(lwide // LANES):
        block = jnp.concatenate(
            [lperm[pl.ds(g * PACK + a, CH, stride=I), :] for a in range(PACK)], axis=0)
        left_out[:, g * LANES:(g + 1) * LANES] = block.T

    if share:
        send(pgather.at[core], pgather.at[1 - core], s_pe, r_pe, other, col).wait_recv()
        proj_out[...] = pgather[...].astype(F32).reshape(2 * half, PAIR)

    for copy in pending:
        copy.wait_send()


def solution(mesh):
    R, C = mesh.shape["row"], mesh.shape["col"]

    def step(left, right, proj, bias, pair_grad):
        lseq, lwide = left.shape
        rseq, rwide = right.shape
        seqs = lseq * C
        outer_size = proj.shape[0]
        I, J = lwide // CH, rwide // CH
        JL = LANES // I
        JH = J // JL
        pairs = I * J
        C2 = inner_size(C)
        C1 = C // C2
        lchunk = lwide // PARTS
        share = outer_size // (R * C) if R % 2 == 0 else 0
        if share % 16:
            share = 0
        half = outer_size // 2
        keep = share or half
        count = half // keep
        some = max(count - 1, 1)
        dma = pltpu.SemaphoreType.DMA
        V = pltpu.VMEM
        scratch = [
            V((PARTS, C, lseq, lchunk), BF16), V((R, rseq, rwide), BF16), V((lchunk, seqs), F32),
            V((CH * LANES, JL * seqs), BF16), V((rwide, seqs), F32), V((JH * CH, JL * seqs), BF16),
            V((JL * seqs, JH * CH), BF16), V((PAIR, outer_size), BF16), V((pairs, PAIR), F32),
            V((PAIR, pairs), F32), V((PAIR, pairs), F32), V((outer_size, pairs), BF16),
            V((PAIR, pairs), BF16), V((JH * CH, CH * LANES), BF16), V((lwide, lseq), F32),
            V((outer_size, PAIR), F32), V((half, PAIR), BF16), V((half, PAIR), BF16),
            V((count, keep, PAIR), F32), V((count, keep, PAIR), BF16),
            V((some, keep, PAIR), BF16), V((2, count, keep, PAIR), BF16),
            V((rwide, seqs), F32), V((R, rseq, rwide), F32), V((R, rseq, rwide), BF16),
            V((R - 1, rseq, rwide), BF16),
            V((PARTS, C, lseq, lchunk), F32), V((PARTS, C, lseq, lchunk), BF16),
            V((PARTS, C2 - 1, C1, lseq, lchunk), BF16), V((PARTS, C1 - 1, lseq, lchunk), BF16),
            V((PARTS, C1 - 1, lseq, lchunk), BF16),
            dma((PARTS, C1 - 1)), dma((PARTS, C1 - 1)),
            dma((PARTS, C2 - 1, C1)), dma((PARTS, C2 - 1, C1)),
            dma((R - 1,)), dma((R - 1,)),
            dma, dma, dma((some,)), dma((some,)), dma((some,)), dma((some,)), dma, dma,
            dma((R - 1,)), dma((R - 1,)),
            dma((PARTS, C2 - 1, C1)), dma((PARTS, C2 - 1, C1)),
            dma((PARTS, C1 - 1)), dma((PARTS, C1 - 1)),
        ]
        vmem = pl.BlockSpec(memory_space=pltpu.VMEM)
        pair_out, left_grad, right_grad, proj_grad = pl.pallas_call(
            functools.partial(kernel, R, C, share),
            out_shape=(
                jax.ShapeDtypeStruct(pair_grad.shape, BF16),
                jax.ShapeDtypeStruct(left.shape, F32),
                jax.ShapeDtypeStruct(right.shape, F32),
                jax.ShapeDtypeStruct(proj.shape, F32),
            ),
            in_specs=[vmem] * 5,
            out_specs=[vmem] * 4,
            scratch_shapes=scratch,
            compiler_params=pltpu.CompilerParams(
                collective_id=0, has_side_effects=True, vmem_limit_bytes=60 << 20),
        )(left, right, proj, bias.reshape(1, -1), pair_grad)
        if not share:
            proj_grad = lax.psum(proj_grad, ("row", "col"))
        return pair_out, left_grad, right_grad, proj_grad

    return jax.shard_map(
        step,
        mesh=mesh,
        in_specs=(P("col", "row"), P("row", "col"), P(), P(), P("row", "col", None)),
        out_specs=(P("row", "col", None), P("col", "row"), P("row", "col"), P()),
        check_vma=False,
    )
```

```python
import functools

import jax
import jax.numpy as jnp
from jax import lax
from jax.experimental import pallas as pl
from jax.experimental.pallas import tpu as pltpu
from jax.sharding import PartitionSpec as P

CH = 32
PAIR = 128
LANES = 128
PACK = LANES // CH
TILE = 256
LONG = 512
PARTS = 2
STEPS = 4
MESH = pl.DeviceIdType.MESH
F32 = jnp.float32
BF16 = jnp.bfloat16


def inner_size(n):
    inner = 1
    while inner * inner * 4 <= n and n % (inner * 2) == 0:
        inner *= 2
    return inner


def dot(a, b):
    return jnp.dot(a, b, preferred_element_type=F32)


def dot_t(a, b):
    return lax.dot_general(a, b, (((1,), (1,)), ((), ())), preferred_element_type=F32)


def aligned(index, size):
    return pl.ds(pl.multiple_of(index * size, size), size)


def fold(tiles, low, width):
    if len(tiles) == 1:
        return tiles[0][0]
    same = jnp.where(low, tiles[0][0], tiles[1][1])
    crossed = jnp.where(low, tiles[1][0], tiles[0][1])
    return same + pltpu.roll(crossed, width, 1)


def kernel(
    R, C, share,
    left, right, proj, bias, pair_grad,
    pair_out, left_out, right_out, proj_out,
    projv, biasv, gradv,
    lbuf, rbuf, ltrans, bt, rtrans, r2, r2t, projt, pairs_f, pgt, sq, outer, gpre, gouter, lperm,
    pterm, psend, precv, psum, pshare, pparts, pmid, pcross, pgather,
    rtmp, rown, rsend, rparts, lown, lsend, lxparts, lzsend, lzparts,
    s_lz, r_lz, s_lx, r_lx, s_rg, r_rg,
    s_pc, r_pc, s_ps, r_ps, s_px, r_px, s_pa, r_pa, s_pe, r_pe,
    s_rs, r_rs, s_lsx, r_lsx, s_lsz, r_lsz, s_left, s_in,
):
    C2 = inner_size(C)
    C1 = C // C2
    row, col = lax.axis_index("row"), lax.axis_index("col")
    z, x = col // C2, lax.rem(col, C2)
    lseq, lwide = left.shape
    seqs = lseq * C
    rwide = right.shape[1]
    I, J = lwide // CH, rwide // CH
    JL = LANES // I
    JH = J // JL
    pairs = I * J
    scale = 1.0 / seqs

    def send(src, dst, ssem, rsem, to_row, to_col):
        return pltpu.make_async_remote_copy(
            src_ref=src, dst_ref=dst, send_sem=ssem, recv_sem=rsem,
            device_id=(to_row, to_col), device_id_type=MESH,
        )

    def zpeer(d):
        return lax.rem(z + d, C1)

    def xpeer(d):
        return lax.rem(x + d, C2)

    def rpeer(d):
        return lax.rem(row + d, R)

    barrier = pltpu.get_barrier_semaphore()
    for d in range(1, R):
        pl.semaphore_signal(barrier, inc=1, device_id=(rpeer(d), col), device_id_type=MESH)
    for d in range(1, C2):
        pl.semaphore_signal(
            barrier, inc=1, device_id=(row, z * C2 + xpeer(d)), device_id_type=MESH)
    for d in range(1, C1):
        pl.semaphore_signal(
            barrier, inc=1, device_id=(row, zpeer(d) * C2 + x), device_id_type=MESH)
    lchunk = lwide // PARTS
    first = [
        pltpu.make_async_copy(
            left.at[:, p * lchunk:(p + 1) * lchunk], lbuf.at[p, col], s_left.at[p])
        for p in range(PARTS)
    ] + [pltpu.make_async_copy(right, rbuf.at[row], s_left.at[PARTS])]
    later = [
        pltpu.make_async_copy(proj, projv, s_in.at[0]),
        pltpu.make_async_copy(bias, biasv, s_in.at[1]),
        pltpu.make_async_copy(pair_grad, gradv, s_in.at[2]),
    ]
    for copy in first + later:
        copy.start()
    pl.semaphore_wait(barrier, R - 1 + C1 - 1 + C2 - 1)

    for copy in first + later:
        copy.wait()

    pending = []

    def go(copy):
        copy.start()
        pending.append(copy)
        return copy

    for p in range(PARTS):
        piece = lbuf.at[p, col]
        for d in range(1, C1):
            go(send(
                piece, piece, s_lz.at[p, d - 1], r_lz.at[p, d - 1],
                row, zpeer(d) * C2 + x))
        for d in range(1, C2):
            go(send(
                piece, piece, s_lx.at[p, d - 1, 0], r_lx.at[p, d - 1, 0],
                row, z * C2 + xpeer(d)))
        if p == 0:
            for d in range(1, R):
                go(send(rbuf.at[row], rbuf.at[row], s_rg.at[d - 1], r_rg.at[d - 1], rpeer(d), col))

    bt[...] = jnp.zeros_like(bt)
    projt[...] = projv[...].astype(F32).T.astype(BF16)
    pairs_f[...] = gradv[...].astype(F32).reshape(pairs, PAIR)
    bias_t = jnp.broadcast_to(biasv[...], (LANES, PAIR)).T

    @pl.loop(0, JH, unroll=True)
    def _(h):
        block = jnp.concatenate(
            [pairs_f[pl.ds(h * JL + a, I, stride=J), :] for a in range(JL)], axis=0)
        pgt[:, aligned(h, LANES)] = block.T

    def pass_on(p):
        for d in range(1, C1):
            block = lax.rem(z + C1 - d, C1) * C2 + x
            send(
                lbuf.at[p, block], lbuf.at[p, block], s_lz.at[p, d - 1], r_lz.at[p, d - 1],
                row, col).wait_recv()
            for k in range(1, C2):
                go(send(
                    lbuf.at[p, block], lbuf.at[p, block], s_lx.at[p, k - 1, d],
                    r_lx.at[p, k - 1, d], row, z * C2 + xpeer(k)))

    ipart = I // PARTS

    def arrive(p):
        for d in range(C1):
            for k in range(1, C2):
                block = lax.rem(z + C1 - d, C1) * C2 + lax.rem(x + C2 - k, C2)
                send(
                    lbuf.at[p, block], lbuf.at[p, block], s_lx.at[p, k - 1, d],
                    r_lx.at[p, k - 1, d], row, col).wait_recv()
        ltrans[...] = lbuf[p].astype(F32).reshape(seqs, lchunk).T

        @pl.loop(0, CH, unroll=True)
        def _(c):
            block = ltrans[pl.ds(c, ipart, stride=CH), :].astype(BF16)
            for a in range(JL):
                bt[
                    pl.ds(pl.multiple_of(c * LANES + a * I + p * ipart, ipart), ipart),
                    a * seqs:(a + 1) * seqs
                ] = block

    pass_on(0)
    for d in range(1, R):
        source = lax.rem(row + R - d, R)
        send(rbuf.at[row], rbuf.at[source], s_rg.at[d - 1], r_rg.at[d - 1], row, col).wait_recv()

    rtrans[...] = rbuf[...].astype(F32).reshape(seqs, rwide).T * scale
    for h in range(JH):
        for a in range(JL):
            at = (h * JL + a) * CH
            r2[h * CH:(h + 1) * CH, a * seqs:(a + 1) * seqs] = rtrans[at:at + CH, :].astype(BF16)
    r2t[...] = r2[...].astype(F32).T.astype(BF16)

    for p in range(PARTS):
        arrive(p)
        if p + 1 < PARTS:
            pass_on(p + 1)

    per = LONG // LANES

    @pl.loop(0, CH * LANES // LONG, unroll=True)
    def _(t):
        part = dot_t(r2[...], bt[aligned(t, LONG), :]).astype(BF16)
        for k in range(per):
            for h in range(JH):
                outer[aligned(t * per + k, CH), h * LANES:(h + 1) * LANES] = (
                    part[h * CH:(h + 1) * CH, k * LANES:(k + 1) * LANES])

    wide_bias = jnp.concatenate([bias_t] * per, axis=1)

    @pl.loop(0, pairs // LONG, unroll=True)
    def _(t):
        here = aligned(t, LONG)
        active = jnp.maximum(dot(projt[...], outer[:, here]) + wide_bias, 0.0)
        sq[:, here] = active * active
        gpre[:, here] = (pgt[:, here] * 2.0 * active).astype(BF16)

    half = pterm.shape[0] // 2
    core = lax.rem(row, 2)

    def proj_term(at):
        @pl.loop(0, half // TILE, unroll=True)
        def _(t):
            rows = pl.ds(pl.multiple_of(at * half + t * TILE, TILE), TILE)
            pterm[rows, :] = dot_t(outer[rows, :], gpre[...])

    low = lax.broadcasted_iota(jnp.int32, (seqs, LANES), 1) < I
    inner = {}
    cpart = CH // STEPS

    def left_part(p):
        @pl.loop(0, cpart * CH // LANES, unroll=True)
        def _(t):
            part = dot(projv[aligned(p * (cpart * CH // LANES) + t, LANES), :], gpre[...]).astype(BF16)
            for k in range(PACK):
                c = (p * (cpart // PACK) + t) * PACK + k
                for h in range(JH):
                    gouter[h * CH:(h + 1) * CH, aligned(c, LANES)] = (
                        part[k * CH:(k + 1) * CH, h * LANES:(h + 1) * LANES])

        @pl.loop(0, cpart * LANES // LONG, unroll=True)
        def _(t):
            part = dot(r2t[...], gouter[:, aligned(p * (cpart * LANES // LONG) + t, LONG)])
            done = []
            for g in range(LONG // LANES // JL):
                tiles = [
                    [
                        part[b * seqs:(b + 1) * seqs, (g * JL + k) * LANES:(g * JL + k + 1) * LANES]
                        for b in range(JL)
                    ]
                    for k in range(JL)
                ]
                done.append(fold(tiles, low, I))
            total = jnp.concatenate(done, axis=1).reshape(C, lseq, LONG // JL)
            lown[p, :, :, aligned(t, LONG // JL)] = total
            lsend[p, :, :, aligned(t, LONG // JL)] = total.astype(BF16)

    def left_send(p):
        for d in list(range(1, C1)) + [0]:
            for k in range(1, C2):
                inner[p, d, k] = go(send(
                    lsend.at[p, zpeer(d) * C2 + xpeer(k)], lxparts.at[p, k - 1, d],
                    s_lsx.at[p, k - 1, d], r_lsx.at[p, k - 1, d], row, z * C2 + xpeer(k)))

    if share:
        other = row + 1 - 2 * core
        count = half // share
        far = z // 2
        me = ((row // 2) * 2 + lax.rem(z, 2)) * C2 + x
        proj_term(1 - core)
        psend[...] = pterm[aligned(1 - core, half), :].astype(BF16)
        swap = go(send(psend, precv, s_pc, r_pc, other, col))
        proj_term(core)

        def owner(k):
            near = lax.rem(k // C2, 2)
            return (k // (2 * C2)) * 2 + core, (far * 2 + near) * C2 + lax.rem(k, C2)

        def spread_sum():
            swap.wait_recv()
            both = (pterm[aligned(core, half), :] + precv[...].astype(F32)).reshape(count, share, PAIR)
            psum[...] = both
            pshare[...] = both.astype(BF16)
            scatter = []
            for d in range(1, count):
                k = lax.rem(me + d, count)
                scatter.append(go(send(
                    pshare.at[k], pparts.at[d - 1], s_ps.at[d - 1], r_ps.at[d - 1], *owner(k))))
            return scatter

        def cross():
            for copy in scatter:
                copy.wait_recv()
            total = psum[me]
            for d in range(1, count):
                total = total + pparts[d - 1].astype(F32)
            pmid[...] = total.astype(BF16)
            return go(send(
                pmid, pcross, s_px, r_px, row, ((1 - far) * 2 + lax.rem(z, 2)) * C2 + x))

        def share_out(copy):
            copy.wait_recv()
            pgather[core, me] = (pmid[...].astype(F32) + pcross[...].astype(F32)).astype(BF16)
            for d in range(1, count):
                k = lax.rem(me + d, count)
                go(send(
                    pgather.at[core, me], pgather.at[core, me], s_pa.at[d - 1], r_pa.at[d - 1],
                    *owner(k)))
    else:
        proj_term(0)
        proj_term(1)

    left_part(0)
    if share:
        scatter = spread_sum()
    left_send(0)
    for p in range(1, STEPS):
        left_part(p)
        left_send(p)

    @pl.loop(0, JH * CH // TILE, unroll=True)
    def _(t):
        part = dot(gouter[aligned(t, TILE), :], bt[...]) * scale
        for h in range(TILE // CH):
            for a in range(JL):
                rtmp[aligned((t * (TILE // CH) + h) * JL + a, CH), :] = (
                    part[h * CH:(h + 1) * CH, a * seqs:(a + 1) * seqs])

    turned = rtmp[...].T.reshape(R, seqs // R, rwide)
    rown[...] = turned
    rsend[...] = turned.astype(BF16)
    rights = [
        go(send(rsend.at[rpeer(d)], rparts.at[d - 1], s_rs.at[d - 1], r_rs.at[d - 1], rpeer(d), col))
        for d in range(1, R)
    ]

    outers = {}

    def pass_sums(p):
        for d in range(1, C1):
            total = lown[p, zpeer(d) * C2 + x]
            for k in range(1, C2):
                inner[p, d, k].wait_recv()
                total = total + lxparts[p, k - 1, d].astype(F32)
            lzsend[p, d - 1] = total.astype(BF16)
            outers[p, d] = go(send(
                lzsend.at[p, d - 1], lzparts.at[p, d - 1], s_lsz.at[p, d - 1],
                r_lsz.at[p, d - 1], row, zpeer(d) * C2 + x))

    pass_sums(0)
    if share:
        crossed = cross()
    else:
        proj_out[...] = pterm[...]
    pass_sums(1)

    @pl.loop(0, JH, unroll=True)
    def _(h):
        block = sq[:, aligned(h, LANES)].T
        for a in range(JL):
            pairs_f[pl.ds(h * JL + a, I, stride=J), :] = block[a * I:(a + 1) * I, :]

    pair_out[...] = pairs_f[...].reshape(I, J, PAIR).astype(BF16)

    if share:
        share_out(crossed)
    for p in range(2, STEPS):
        pass_sums(p)

    for copy in rights:
        copy.wait_recv()
    total = rown[row]
    for d in range(1, R):
        total = total + rparts[d - 1].astype(F32)
    right_out[...] = total

    if share:
        for d in range(1, count):
            k = lax.rem(me + count - d, count)
            send(
                pgather.at[core, me], pgather.at[core, k], s_pa.at[d - 1], r_pa.at[d - 1],
                *owner(k)).wait_recv()
        swap = go(send(pgather.at[core], pgather.at[core], s_pe, r_pe, other, col))

    lstep = lwide // STEPS
    for p in range(STEPS):
        total = lown[p, col]
        for k in range(1, C2):
            inner[p, 0, k].wait_recv()
            total = total + lxparts[p, k - 1, 0].astype(F32)
        for d in range(1, C1):
            outers[p, d].wait_recv()
            total = total + lzparts[p, d - 1].astype(F32)
        lperm[p * lstep:(p + 1) * lstep, :] = total.T
    for g in range(lwide // LANES):
        block = jnp.concatenate(
            [lperm[pl.ds(g * PACK + a, CH, stride=I), :] for a in range(PACK)], axis=0)
        left_out[:, g * LANES:(g + 1) * LANES] = block.T

    if share:
        send(pgather.at[core], pgather.at[1 - core], s_pe, r_pe, other, col).wait_recv()
        proj_out[...] = pgather[...].reshape(2 * half, PAIR)

    for copy in pending:
        copy.wait_send()


def finish(pair, left, right, proj, pair_out, left_out, right_out, proj_out, wide, sems):
    ends = ((pair, pair_out), (left, left_out), (right, right_out), (wide, proj_out))
    stores = [pltpu.make_async_copy(src, dst, sems.at[k]) for k, (src, dst) in enumerate(ends)]
    for copy in stores[:3]:
        copy.start()
    wide[...] = proj[...].astype(F32)
    stores[3].start()
    for copy in stores:
        copy.wait()


def solution(mesh):
    R, C = mesh.shape["row"], mesh.shape["col"]

    def step(left, right, proj, bias, pair_grad):
        lseq, lwide = left.shape
        rseq, rwide = right.shape
        seqs = lseq * C
        outer_size = proj.shape[0]
        I, J = lwide // CH, rwide // CH
        JL = LANES // I
        JH = J // JL
        pairs = I * J
        C2 = inner_size(C)
        C1 = C // C2
        lchunk = lwide // PARTS
        lstep = lwide // STEPS
        half = outer_size // 2
        share = half // (R * C2) if R % 2 == 0 and C1 == 4 else 0
        if share % 16:
            share = 0
        keep = share or half
        count = half // keep
        some = max(count - 1, 1)
        dma = pltpu.SemaphoreType.DMA
        V = pltpu.VMEM
        scratch = [
            V(proj.shape, BF16), V((1, PAIR), F32), V(pair_grad.shape, BF16),
            V((PARTS, C, lseq, lchunk), BF16), V((R, rseq, rwide), BF16), V((lchunk, seqs), F32),
            V((CH * LANES, JL * seqs), BF16), V((rwide, seqs), F32), V((JH * CH, JL * seqs), BF16),
            V((JL * seqs, JH * CH), BF16), V((PAIR, outer_size), BF16), V((pairs, PAIR), F32),
            V((PAIR, pairs), F32), V((PAIR, pairs), F32), V((outer_size, pairs), BF16),
            V((PAIR, pairs), BF16), V((JH * CH, CH * LANES), BF16), V((lwide, lseq), F32),
            V((outer_size, PAIR), F32), V((half, PAIR), BF16), V((half, PAIR), BF16),
            V((count, keep, PAIR), F32), V((count, keep, PAIR), BF16),
            V((some, keep, PAIR), BF16), V((keep, PAIR), BF16), V((keep, PAIR), BF16),
            V((2, count, keep, PAIR), BF16),
            V((rwide, seqs), F32), V((R, rseq, rwide), F32), V((R, rseq, rwide), BF16),
            V((R - 1, rseq, rwide), BF16),
            V((STEPS, C, lseq, lstep), F32), V((STEPS, C, lseq, lstep), BF16),
            V((STEPS, C2 - 1, C1, lseq, lstep), BF16), V((STEPS, C1 - 1, lseq, lstep), BF16),
            V((STEPS, C1 - 1, lseq, lstep), BF16),
            dma((PARTS, C1 - 1)), dma((PARTS, C1 - 1)),
            dma((PARTS, C2 - 1, C1)), dma((PARTS, C2 - 1, C1)),
            dma((R - 1,)), dma((R - 1,)),
            dma, dma, dma((some,)), dma((some,)), dma, dma, dma((some,)), dma((some,)), dma, dma,
            dma((R - 1,)), dma((R - 1,)),
            dma((STEPS, C2 - 1, C1)), dma((STEPS, C2 - 1, C1)),
            dma((STEPS, C1 - 1)), dma((STEPS, C1 - 1)),
            dma((PARTS + 1,)), dma((3,)),
        ]
        vmem = pl.BlockSpec(memory_space=pltpu.VMEM)
        hbm = pl.BlockSpec(memory_space=pl.ANY)
        pair_out, left_grad, right_grad, proj_grad = pl.pallas_call(
            functools.partial(kernel, R, C, share),
            out_shape=(
                V(pair_grad.shape, BF16), V(left.shape, F32), V(right.shape, F32),
                V(proj.shape, BF16 if share else F32),
            ),
            in_specs=[hbm] * 5,
            out_specs=[vmem] * 4,
            scratch_shapes=scratch,
            compiler_params=pltpu.CompilerParams(
                collective_id=0, has_side_effects=True, vmem_limit_bytes=60 << 20),
        )(left, right, proj, bias.reshape(1, -1), pair_grad)
        if not share:
            proj_grad = lax.psum(proj_grad, ("row", "col"))
        return pl.pallas_call(
            finish,
            out_shape=(
                jax.ShapeDtypeStruct(pair_grad.shape, BF16),
                jax.ShapeDtypeStruct(left.shape, F32),
                jax.ShapeDtypeStruct(right.shape, F32),
                jax.ShapeDtypeStruct(proj.shape, F32),
            ),
            in_specs=[vmem] * 4,
            out_specs=[hbm] * 4,
            scratch_shapes=[V(proj.shape, F32), dma((4,))],
        )(*(
            pltpu.with_memory_space_constraint(part, pltpu.VMEM)
            for part in (pair_out, left_grad, right_grad, proj_grad)
        ))

    return jax.shard_map(
        step,
        mesh=mesh,
        in_specs=(P("col", "row"), P("row", "col"), P(), P(), P("row", "col", None)),
        out_specs=(P("row", "col", None), P("col", "row"), P("row", "col"), P()),
        check_vma=False,
    )
```

```python
import functools

import jax
import jax.numpy as jnp
from jax import lax
from jax.experimental import pallas as pl
from jax.experimental.pallas import tpu as pltpu
from jax.sharding import PartitionSpec as P

CH = 32
PAIR = 128
LANES = 128
PACK = LANES // CH
TILE = 256
LONG = 512
PARTS = 2
STEPS = 4
MESH = pl.DeviceIdType.MESH
F32 = jnp.float32
BF16 = jnp.bfloat16


def inner_size(n):
    inner = 1
    while inner * inner * 4 <= n and n % (inner * 2) == 0:
        inner *= 2
    return inner


def dot(a, b):
    return jnp.dot(a, b, preferred_element_type=F32)


def dot_t(a, b):
    return lax.dot_general(a, b, (((1,), (1,)), ((), ())), preferred_element_type=F32)


def aligned(index, size):
    return pl.ds(pl.multiple_of(index * size, size), size)


def fold(tiles, low, width):
    if len(tiles) == 1:
        return tiles[0][0]
    same = jnp.where(low, tiles[0][0], tiles[1][1])
    crossed = jnp.where(low, tiles[1][0], tiles[0][1])
    return same + pltpu.roll(crossed, width, 1)


def kernel(
    R, C, share,
    left, right, proj, bias, pair_grad,
    pair_out, left_out, right_out, proj_out,
    projv, biasv, gradv, lraw,
    lbuf, rbuf, bt, rtrans, r2, r2t, projt, pairs_f, pgt, sq, outer, gpre, gouter, lperm,
    pterm, psend, precv, psum, pshare, pparts, pmid, pcross, pgather,
    rtmp, rown, rsend, rparts, lown, lsend, lxparts, lzsend, lzparts,
    s_lz, r_lz, s_lx, r_lx, s_rg, r_rg,
    s_pc, r_pc, s_ps, r_ps, s_px, r_px, s_pa, r_pa, s_pe, r_pe,
    s_rs, r_rs, s_lsx, r_lsx, s_lsz, r_lsz, s_left, s_in,
):
    C2 = inner_size(C)
    C1 = C // C2
    row, col = lax.axis_index("row"), lax.axis_index("col")
    z, x = col // C2, lax.rem(col, C2)
    lseq, lwide = left.shape
    seqs = lseq * C
    rwide = right.shape[1]
    I, J = lwide // CH, rwide // CH
    JL = LANES // I
    JH = J // JL
    pairs = I * J
    scale = 1.0 / seqs

    def send(src, dst, ssem, rsem, to_row, to_col):
        return pltpu.make_async_remote_copy(
            src_ref=src, dst_ref=dst, send_sem=ssem, recv_sem=rsem,
            device_id=(to_row, to_col), device_id_type=MESH,
        )

    def zpeer(d):
        return lax.rem(z + d, C1)

    def xpeer(d):
        return lax.rem(x + d, C2)

    def rpeer(d):
        return lax.rem(row + d, R)

    barrier = pltpu.get_barrier_semaphore()
    for d in range(1, R):
        pl.semaphore_signal(barrier, inc=1, device_id=(rpeer(d), col), device_id_type=MESH)
    for d in range(1, C2):
        pl.semaphore_signal(
            barrier, inc=1, device_id=(row, z * C2 + xpeer(d)), device_id_type=MESH)
    for d in range(1, C1):
        pl.semaphore_signal(
            barrier, inc=1, device_id=(row, zpeer(d) * C2 + x), device_id_type=MESH)
    lchunk = lwide // PARTS
    first = [
        pltpu.make_async_copy(left, lraw, s_left.at[0]),
        pltpu.make_async_copy(right, rbuf.at[row], s_left.at[1]),
    ]
    later = [
        pltpu.make_async_copy(proj, projv, s_in.at[0]),
        pltpu.make_async_copy(bias, biasv, s_in.at[1]),
        pltpu.make_async_copy(pair_grad, gradv, s_in.at[2]),
    ]
    for copy in first + later:
        copy.start()
    first[0].wait()
    lperm[...] = lraw[...].astype(F32).T
    tiles = lchunk // LANES
    for g in range(lwide // LANES):
        block = jnp.concatenate(
            [lperm[pl.ds(g * JL + a, I, stride=CH), :] for a in range(JL)], axis=0)
        lbuf[g // tiles, col, :, g % tiles * LANES:(g % tiles + 1) * LANES] = block.T.astype(BF16)
    pl.semaphore_wait(barrier, R - 1 + C1 - 1 + C2 - 1)

    first[1].wait()

    pending = []

    def go(copy):
        copy.start()
        pending.append(copy)
        return copy

    def drain(keep=0):
        for copy in pending[:len(pending) - keep]:
            copy.wait_send()
        del pending[:len(pending) - keep]

    for p in range(PARTS):
        piece = lbuf.at[p, col]
        for d in range(1, C1):
            go(send(
                piece, piece, s_lz.at[p, d - 1], r_lz.at[p, d - 1],
                row, zpeer(d) * C2 + x))
        for d in range(1, C2):
            go(send(
                piece, piece, s_lx.at[p, d - 1, 0], r_lx.at[p, d - 1, 0],
                row, z * C2 + xpeer(d)))
        if p == 0:
            for d in range(1, R):
                go(send(rbuf.at[row], rbuf.at[row], s_rg.at[d - 1], r_rg.at[d - 1], rpeer(d), col))

    for copy in later:
        copy.wait()
    bt[...] = jnp.zeros_like(bt)
    projt[...] = projv[...].astype(F32).T.astype(BF16)
    pairs_f[...] = gradv[...].astype(F32).reshape(pairs, PAIR)
    bias_t = jnp.broadcast_to(biasv[...], (LANES, PAIR)).T

    @pl.loop(0, JH, unroll=True)
    def _(h):
        block = jnp.concatenate(
            [pairs_f[pl.ds(h * JL + a, I, stride=J), :] for a in range(JL)], axis=0)
        pgt[:, aligned(h, LANES)] = block.T

    def pass_on(p):
        for d in range(1, C1):
            block = lax.rem(z + C1 - d, C1) * C2 + x
            send(
                lbuf.at[p, block], lbuf.at[p, block], s_lz.at[p, d - 1], r_lz.at[p, d - 1],
                row, col).wait_recv()
            for k in range(1, C2):
                go(send(
                    lbuf.at[p, block], lbuf.at[p, block], s_lx.at[p, k - 1, d],
                    r_lx.at[p, k - 1, d], row, z * C2 + xpeer(k)))

    def arrive(p):
        for d in range(C1):
            for k in range(1, C2):
                block = lax.rem(z + C1 - d, C1) * C2 + lax.rem(x + C2 - k, C2)
                send(
                    lbuf.at[p, block], lbuf.at[p, block], s_lx.at[p, k - 1, d],
                    r_lx.at[p, k - 1, d], row, col).wait_recv()
        turned = lbuf[p].astype(F32).reshape(seqs, lchunk).T.astype(BF16)
        for k in range(CH // PARTS):
            c = p * (CH // PARTS) + k
            for a in range(JL):
                bt[c * LANES + a * I:c * LANES + (a + 1) * I, a * seqs:(a + 1) * seqs] = (
                    turned[k * I:(k + 1) * I, :])

    pass_on(0)
    for d in range(1, R):
        source = lax.rem(row + R - d, R)
        send(rbuf.at[row], rbuf.at[source], s_rg.at[d - 1], r_rg.at[d - 1], row, col).wait_recv()

    rtrans[...] = rbuf[...].astype(F32).reshape(seqs, rwide).T * scale
    for h in range(JH):
        for a in range(JL):
            at = (h * JL + a) * CH
            r2[h * CH:(h + 1) * CH, a * seqs:(a + 1) * seqs] = rtrans[at:at + CH, :].astype(BF16)
    r2t[...] = r2[...].astype(F32).T.astype(BF16)

    for p in range(1, PARTS):
        pass_on(p)

    per = LONG // LANES
    deep = CH * CH // PARTS
    wide_bias = jnp.concatenate([bias_t] * per, axis=1)
    for p in range(PARTS):
        arrive(p)

        @pl.loop(p * CH // PARTS // per, (p + 1) * CH // PARTS // per, unroll=True)
        def _(t):
            part = dot_t(r2[...], bt[aligned(t, LONG), :]).astype(BF16)
            for k in range(per):
                for h in range(JH):
                    outer[aligned(t * per + k, CH), h * LANES:(h + 1) * LANES] = (
                        part[h * CH:(h + 1) * CH, k * LANES:(k + 1) * LANES])

        @pl.loop(0, pairs // LONG, unroll=True)
        def _(t):
            here = aligned(t, LONG)
            part = dot(
                projt[:, p * deep:(p + 1) * deep], outer[p * deep:(p + 1) * deep, here])
            part = part + (wide_bias if p == 0 else sq[:, here])
            if p < PARTS - 1:
                sq[:, here] = part
            else:
                active = jnp.maximum(part, 0.0)
                sq[:, here] = active * active
                gpre[:, here] = (pgt[:, here] * 2.0 * active).astype(BF16)

    half = pterm.shape[0] // 2
    core = lax.rem(row, 2)
    sent = len(pending)

    def proj_term(at):
        @pl.loop(0, half // TILE, unroll=True)
        def _(t):
            rows = pl.ds(pl.multiple_of(at * half + t * TILE, TILE), TILE)
            pterm[rows, :] = dot_t(outer[rows, :], gpre[...])

    low = lax.broadcasted_iota(jnp.int32, (seqs, LANES), 1) < I
    inner = {}
    cpart = CH // STEPS

    def left_part(p):
        @pl.loop(0, cpart * CH // LANES, unroll=True)
        def _(t):
            part = dot(projv[aligned(p * (cpart * CH // LANES) + t, LANES), :], gpre[...]).astype(BF16)
            for k in range(PACK):
                c = (p * (cpart // PACK) + t) * PACK + k
                for h in range(JH):
                    gouter[h * CH:(h + 1) * CH, aligned(c, LANES)] = (
                        part[k * CH:(k + 1) * CH, h * LANES:(h + 1) * LANES])

        @pl.loop(0, cpart * LANES // LONG, unroll=True)
        def _(t):
            part = dot(r2t[...], gouter[:, aligned(p * (cpart * LANES // LONG) + t, LONG)])
            done = []
            for g in range(LONG // LANES // JL):
                tiles = [
                    [
                        part[b * seqs:(b + 1) * seqs, (g * JL + k) * LANES:(g * JL + k + 1) * LANES]
                        for b in range(JL)
                    ]
                    for k in range(JL)
                ]
                done.append(fold(tiles, low, I))
            total = jnp.concatenate(done, axis=1).reshape(C, lseq, LONG // JL)
            lown[p, :, :, aligned(t, LONG // JL)] = total
            lsend[p, :, :, aligned(t, LONG // JL)] = total.astype(BF16)

    def left_send(p):
        for d in list(range(1, C1)) + [0]:
            for k in range(1, C2):
                inner[p, d, k] = go(send(
                    lsend.at[p, zpeer(d) * C2 + xpeer(k)], lxparts.at[p, k - 1, d],
                    s_lsx.at[p, k - 1, d], r_lsx.at[p, k - 1, d], row, z * C2 + xpeer(k)))

    if share:
        other = row + 1 - 2 * core
        count = half // share
        far = z // 2
        me = ((row // 2) * 2 + lax.rem(z, 2)) * C2 + x
        proj_term(1 - core)
        psend[...] = pterm[aligned(1 - core, half), :].astype(BF16)
        swap = go(send(psend, precv, s_pc, r_pc, other, col))
        proj_term(core)

        def owner(k):
            near = lax.rem(k // C2, 2)
            return (k // (2 * C2)) * 2 + core, (far * 2 + near) * C2 + lax.rem(k, C2)

        def spread_sum():
            swap.wait_recv()
            both = (pterm[aligned(core, half), :] + precv[...].astype(F32)).reshape(count, share, PAIR)
            psum[...] = both
            pshare[...] = both.astype(BF16)
            scatter = []
            for d in range(1, count):
                k = lax.rem(me + d, count)
                scatter.append(go(send(
                    pshare.at[k], pparts.at[d - 1], s_ps.at[d - 1], r_ps.at[d - 1], *owner(k))))
            return scatter

        def cross():
            for copy in scatter:
                copy.wait_recv()
            total = psum[me]
            for d in range(1, count):
                total = total + pparts[d - 1].astype(F32)
            pmid[...] = total.astype(BF16)
            return go(send(
                pmid, pcross, s_px, r_px, row, ((1 - far) * 2 + lax.rem(z, 2)) * C2 + x))

        def share_out(copy):
            copy.wait_recv()
            pgather[core, me] = (pmid[...].astype(F32) + pcross[...].astype(F32)).astype(BF16)
            for d in range(1, count):
                k = lax.rem(me + d, count)
                go(send(
                    pgather.at[core, me], pgather.at[core, me], s_pa.at[d - 1], r_pa.at[d - 1],
                    *owner(k)))
    else:
        proj_term(0)
        proj_term(1)

    left_part(0)
    if share:
        scatter = spread_sum()
    left_send(0)
    for p in range(1, STEPS):
        left_part(p)
        left_send(p)

    @pl.loop(0, JH * CH // TILE, unroll=True)
    def _(t):
        part = dot(gouter[aligned(t, TILE), :], bt[...]) * scale
        for h in range(TILE // CH):
            for a in range(JL):
                rtmp[aligned((t * (TILE // CH) + h) * JL + a, CH), :] = (
                    part[h * CH:(h + 1) * CH, a * seqs:(a + 1) * seqs])

    turned = rtmp[...].T.reshape(R, seqs // R, rwide)
    rown[...] = turned
    rsend[...] = turned.astype(BF16)
    rights = [
        go(send(rsend.at[rpeer(d)], rparts.at[d - 1], s_rs.at[d - 1], r_rs.at[d - 1], rpeer(d), col))
        for d in range(1, R)
    ]

    outers = {}

    def pass_sums(p):
        for d in range(1, C1):
            total = lown[p, zpeer(d) * C2 + x]
            for k in range(1, C2):
                inner[p, d, k].wait_recv()
                total = total + lxparts[p, k - 1, d].astype(F32)
            lzsend[p, d - 1] = total.astype(BF16)
            outers[p, d] = go(send(
                lzsend.at[p, d - 1], lzparts.at[p, d - 1], s_lsz.at[p, d - 1],
                r_lsz.at[p, d - 1], row, zpeer(d) * C2 + x))

    drain(len(pending) - sent)
    if share:
        crossed = cross()
    else:
        proj_out[...] = pterm[...]
    pass_sums(0)
    pass_sums(1)

    @pl.loop(0, JH, unroll=True)
    def _(h):
        block = sq[:, aligned(h, LANES)].T
        for a in range(JL):
            pairs_f[pl.ds(h * JL + a, I, stride=J), :] = block[a * I:(a + 1) * I, :]

    pair_out[...] = pairs_f[...].reshape(I, J, PAIR).astype(BF16)

    if share:
        share_out(crossed)
    for p in range(2, STEPS):
        pass_sums(p)

    for copy in rights:
        copy.wait_recv()
    total = rown[row]
    for d in range(1, R):
        total = total + rparts[d - 1].astype(F32)
    right_out[...] = total

    lstep = lwide // STEPS

    def left_sum(p):
        total = lown[p, col]
        for k in range(1, C2):
            inner[p, 0, k].wait_recv()
            total = total + lxparts[p, k - 1, 0].astype(F32)
        for d in range(1, C1):
            outers[p, d].wait_recv()
            total = total + lzparts[p, d - 1].astype(F32)
        lperm[p * lstep:(p + 1) * lstep, :] = total.T

    for p in range(STEPS - 1):
        left_sum(p)
    drain(3)

    if share:
        for d in range(1, count):
            k = lax.rem(me + count - d, count)
            send(
                pgather.at[core, me], pgather.at[core, k], s_pa.at[d - 1], r_pa.at[d - 1],
                *owner(k)).wait_recv()
        swap = go(send(pgather.at[core], pgather.at[core], s_pe, r_pe, other, col))

    left_sum(STEPS - 1)
    for g in range(lwide // LANES):
        block = jnp.concatenate(
            [lperm[pl.ds(g * PACK + a, CH, stride=I), :] for a in range(PACK)], axis=0)
        left_out[:, g * LANES:(g + 1) * LANES] = block.T

    if share:
        send(pgather.at[core], pgather.at[1 - core], s_pe, r_pe, other, col).wait_recv()
        proj_out[...] = pgather[...].reshape(2 * half, PAIR)

    drain()


def finish(pair, left, right, proj, pair_out, left_out, right_out, proj_out, wide, sems):
    ends = ((pair, pair_out), (left, left_out), (right, right_out), (wide, proj_out))
    stores = [pltpu.make_async_copy(src, dst, sems.at[k]) for k, (src, dst) in enumerate(ends)]
    for copy in stores[:3]:
        copy.start()
    wide[...] = proj[...].astype(F32)
    stores[3].start()
    for copy in stores:
        copy.wait()


def solution(mesh):
    R, C = mesh.shape["row"], mesh.shape["col"]

    def step(left, right, proj, bias, pair_grad):
        lseq, lwide = left.shape
        rseq, rwide = right.shape
        seqs = lseq * C
        outer_size = proj.shape[0]
        I, J = lwide // CH, rwide // CH
        JL = LANES // I
        JH = J // JL
        pairs = I * J
        C2 = inner_size(C)
        C1 = C // C2
        lchunk = lwide // PARTS
        lstep = lwide // STEPS
        half = outer_size // 2
        share = half // (R * C2) if R % 2 == 0 and C1 == 4 else 0
        if share % 16:
            share = 0
        keep = share or half
        count = half // keep
        some = max(count - 1, 1)
        dma = pltpu.SemaphoreType.DMA
        V = pltpu.VMEM
        scratch = [
            V(proj.shape, BF16), V((1, PAIR), F32), V(pair_grad.shape, BF16), V(left.shape, BF16),
            V((PARTS, C, lseq, lchunk), BF16), V((R, rseq, rwide), BF16),
            V((CH * LANES, JL * seqs), BF16), V((rwide, seqs), F32), V((JH * CH, JL * seqs), BF16),
            V((JL * seqs, JH * CH), BF16), V((PAIR, outer_size), BF16), V((pairs, PAIR), F32),
            V((PAIR, pairs), F32), V((PAIR, pairs), F32), V((outer_size, pairs), BF16),
            V((PAIR, pairs), BF16), V((JH * CH, CH * LANES), BF16), V((lwide, lseq), F32),
            V((outer_size, PAIR), F32), V((half, PAIR), BF16), V((half, PAIR), BF16),
            V((count, keep, PAIR), F32), V((count, keep, PAIR), BF16),
            V((some, keep, PAIR), BF16), V((keep, PAIR), BF16), V((keep, PAIR), BF16),
            V((2, count, keep, PAIR), BF16),
            V((rwide, seqs), F32), V((R, rseq, rwide), F32), V((R, rseq, rwide), BF16),
            V((R - 1, rseq, rwide), BF16),
            V((STEPS, C, lseq, lstep), F32), V((STEPS, C, lseq, lstep), BF16),
            V((STEPS, C2 - 1, C1, lseq, lstep), BF16), V((STEPS, C1 - 1, lseq, lstep), BF16),
            V((STEPS, C1 - 1, lseq, lstep), BF16),
            dma((PARTS, C1 - 1)), dma((PARTS, C1 - 1)),
            dma((PARTS, C2 - 1, C1)), dma((PARTS, C2 - 1, C1)),
            dma((R - 1,)), dma((R - 1,)),
            dma, dma, dma((some,)), dma((some,)), dma, dma, dma((some,)), dma((some,)), dma, dma,
            dma((R - 1,)), dma((R - 1,)),
            dma((STEPS, C2 - 1, C1)), dma((STEPS, C2 - 1, C1)),
            dma((STEPS, C1 - 1)), dma((STEPS, C1 - 1)),
            dma((2,)), dma((3,)),
        ]
        vmem = pl.BlockSpec(memory_space=pltpu.VMEM)
        hbm = pl.BlockSpec(memory_space=pl.ANY)
        pair_out, left_grad, right_grad, proj_grad = pl.pallas_call(
            functools.partial(kernel, R, C, share),
            out_shape=(
                V(pair_grad.shape, BF16), V(left.shape, F32), V(right.shape, F32),
                V(proj.shape, BF16 if share else F32),
            ),
            in_specs=[hbm] * 5,
            out_specs=[vmem] * 4,
            scratch_shapes=scratch,
            compiler_params=pltpu.CompilerParams(
                collective_id=0, has_side_effects=True, vmem_limit_bytes=60 << 20),
        )(left, right, proj, bias.reshape(1, -1), pair_grad)
        if not share:
            proj_grad = lax.psum(proj_grad, ("row", "col"))
        return pl.pallas_call(
            finish,
            out_shape=(
                jax.ShapeDtypeStruct(pair_grad.shape, BF16),
                jax.ShapeDtypeStruct(left.shape, F32),
                jax.ShapeDtypeStruct(right.shape, F32),
                jax.ShapeDtypeStruct(proj.shape, F32),
            ),
            in_specs=[vmem] * 4,
            out_specs=[hbm] * 4,
            scratch_shapes=[V(proj.shape, F32), dma((4,))],
        )(*(
            pltpu.with_memory_space_constraint(part, pltpu.VMEM)
            for part in (pair_out, left_grad, right_grad, proj_grad)
        ))

    return jax.shard_map(
        step,
        mesh=mesh,
        in_specs=(P("col", "row"), P("row", "col"), P(), P(), P("row", "col", None)),
        out_specs=(P("row", "col", None), P("col", "row"), P("row", "col"), P()),
        check_vma=False,
    )
```

```python
import functools

import jax
import jax.numpy as jnp
from jax import lax
from jax.experimental import pallas as pl
from jax.experimental.pallas import tpu as pltpu
from jax.sharding import PartitionSpec as P

CH = 32
PAIR = 128
LANES = 128
PACK = LANES // CH
TILE = 256
LONG = 512
PARTS = 2
STEPS = 4
MESH = pl.DeviceIdType.MESH
F32 = jnp.float32
BF16 = jnp.bfloat16


def inner_size(n):
    inner = 1
    while inner * inner * 4 <= n and n % (inner * 2) == 0:
        inner *= 2
    return inner


def dot(a, b):
    return jnp.dot(a, b, preferred_element_type=F32)


def dot_t(a, b):
    return lax.dot_general(a, b, (((1,), (1,)), ((), ())), preferred_element_type=F32)


def aligned(index, size):
    return pl.ds(pl.multiple_of(index * size, size), size)


def fold(tiles, low, width):
    if len(tiles) == 1:
        return tiles[0][0]
    same = jnp.where(low, tiles[0][0], tiles[1][1])
    crossed = jnp.where(low, tiles[1][0], tiles[0][1])
    return same + pltpu.roll(crossed, width, 1)


def kernel(
    R, C, share,
    left, right, proj, bias, pair_grad,
    pair_out, left_out, right_out, proj_out,
    projv, biasv, gradv, lraw,
    lbuf, rbuf, bt, rtrans, r2, r2t, projt, pairs_f, pgt, sq, outer, gpre, gouter, lperm,
    pterm, psend, precv, psum, pshare, pparts, pmid, pcross, pgather,
    rtmp, rown, rsend, rparts, lown, lsend, lxparts, lzsend, lzparts,
    s_lz, r_lz, s_lx, r_lx, s_rg, r_rg,
    s_pc, r_pc, s_ps, r_ps, s_px, r_px, s_pa, r_pa, s_pe, r_pe,
    s_rs, r_rs, s_lsx, r_lsx, s_lsz, r_lsz, s_left, s_in,
):
    C2 = inner_size(C)
    C1 = C // C2
    row, col = lax.axis_index("row"), lax.axis_index("col")
    z, x = col // C2, lax.rem(col, C2)
    lseq, lwide = left.shape
    seqs = lseq * C
    rwide = right.shape[1]
    I, J = lwide // CH, rwide // CH
    JL = LANES // I
    JH = J // JL
    pairs = I * J
    scale = 1.0 / seqs

    def send(src, dst, ssem, rsem, to_row, to_col):
        return pltpu.make_async_remote_copy(
            src_ref=src, dst_ref=dst, send_sem=ssem, recv_sem=rsem,
            device_id=(to_row, to_col), device_id_type=MESH,
        )

    def zpeer(d):
        return lax.rem(z + d, C1)

    def xpeer(d):
        return lax.rem(x + d, C2)

    def rpeer(d):
        return lax.rem(row + d, R)

    barrier = pltpu.get_barrier_semaphore()
    for d in range(1, R):
        pl.semaphore_signal(barrier, inc=1, device_id=(rpeer(d), col), device_id_type=MESH)
    for d in range(1, C2):
        pl.semaphore_signal(
            barrier, inc=1, device_id=(row, z * C2 + xpeer(d)), device_id_type=MESH)
    for d in range(1, C1):
        pl.semaphore_signal(
            barrier, inc=1, device_id=(row, zpeer(d) * C2 + x), device_id_type=MESH)
    lchunk = lwide // PARTS
    first = [
        pltpu.make_async_copy(left, lraw, s_left.at[0]),
        pltpu.make_async_copy(right, rbuf.at[row], s_left.at[1]),
    ]
    later = [
        pltpu.make_async_copy(proj, projv, s_in.at[0]),
        pltpu.make_async_copy(bias, biasv, s_in.at[1]),
        pltpu.make_async_copy(pair_grad, gradv, s_in.at[2]),
    ]
    for copy in first + later:
        copy.start()
    first[0].wait()
    lperm[...] = lraw[...].astype(F32).T
    tiles = lchunk // LANES
    for g in range(lwide // LANES):
        block = jnp.concatenate(
            [lperm[pl.ds(g * JL + a, I, stride=CH), :] for a in range(JL)], axis=0)
        lbuf[g // tiles, col, :, g % tiles * LANES:(g % tiles + 1) * LANES] = block.T.astype(BF16)
    pl.semaphore_wait(barrier, R - 1 + C1 - 1 + C2 - 1)

    first[1].wait()

    pending = []

    def go(copy):
        copy.start()
        pending.append(copy)
        return copy

    def drain(keep=0):
        for copy in pending[:len(pending) - keep]:
            copy.wait_send()
        del pending[:len(pending) - keep]

    for p in range(PARTS):
        piece = lbuf.at[p, col]
        for d in range(1, C1):
            go(send(
                piece, piece, s_lz.at[p, d - 1], r_lz.at[p, d - 1],
                row, zpeer(d) * C2 + x))
        for d in range(1, C2):
            go(send(
                piece, piece, s_lx.at[p, d - 1, 0], r_lx.at[p, d - 1, 0],
                row, z * C2 + xpeer(d)))
        if p == 0:
            for d in range(1, R):
                go(send(rbuf.at[row], rbuf.at[row], s_rg.at[d - 1], r_rg.at[d - 1], rpeer(d), col))

    for copy in later:
        copy.wait()
    bt[...] = jnp.zeros_like(bt)
    projt[...] = projv[...].astype(F32).T.astype(BF16)
    pairs_f[...] = gradv[...].astype(F32).reshape(pairs, PAIR)
    bias_t = jnp.broadcast_to(biasv[...], (LANES, PAIR)).T

    @pl.loop(0, JH, unroll=True)
    def _(h):
        block = jnp.concatenate(
            [pairs_f[pl.ds(h * JL + a, I, stride=J), :] for a in range(JL)], axis=0)
        pgt[:, aligned(h, LANES)] = block.T

    def pass_on(p):
        for d in range(1, C1):
            block = lax.rem(z + C1 - d, C1) * C2 + x
            send(
                lbuf.at[p, block], lbuf.at[p, block], s_lz.at[p, d - 1], r_lz.at[p, d - 1],
                row, col).wait_recv()
            for k in range(1, C2):
                go(send(
                    lbuf.at[p, block], lbuf.at[p, block], s_lx.at[p, k - 1, d],
                    r_lx.at[p, k - 1, d], row, z * C2 + xpeer(k)))

    def arrive(p):
        for d in range(C1):
            for k in range(1, C2):
                block = lax.rem(z + C1 - d, C1) * C2 + lax.rem(x + C2 - k, C2)
                send(
                    lbuf.at[p, block], lbuf.at[p, block], s_lx.at[p, k - 1, d],
                    r_lx.at[p, k - 1, d], row, col).wait_recv()
        turned = lbuf[p].astype(F32).reshape(seqs, lchunk).T.astype(BF16)
        for k in range(CH // PARTS):
            c = p * (CH // PARTS) + k
            for a in range(JL):
                bt[c * LANES + a * I:c * LANES + (a + 1) * I, a * seqs:(a + 1) * seqs] = (
                    turned[k * I:(k + 1) * I, :])

    pass_on(0)
    for d in range(1, R):
        source = lax.rem(row + R - d, R)
        send(rbuf.at[row], rbuf.at[source], s_rg.at[d - 1], r_rg.at[d - 1], row, col).wait_recv()

    rtrans[...] = rbuf[...].astype(F32).reshape(seqs, rwide).T * scale
    for h in range(JH):
        for a in range(JL):
            at = (h * JL + a) * CH
            r2[h * CH:(h + 1) * CH, a * seqs:(a + 1) * seqs] = rtrans[at:at + CH, :].astype(BF16)
    r2t[...] = r2[...].astype(F32).T.astype(BF16)

    for p in range(1, PARTS):
        pass_on(p)

    per = LONG // LANES
    deep = CH * CH // PARTS
    wide_bias = jnp.concatenate([bias_t] * per, axis=1)
    for p in range(PARTS):
        arrive(p)

        @pl.loop(p * CH // PARTS // per, (p + 1) * CH // PARTS // per, unroll=True)
        def _(t):
            part = dot_t(r2[...], bt[aligned(t, LONG), :]).astype(BF16)
            for k in range(per):
                for h in range(JH):
                    outer[aligned(t * per + k, CH), h * LANES:(h + 1) * LANES] = (
                        part[h * CH:(h + 1) * CH, k * LANES:(k + 1) * LANES])

        @pl.loop(0, pairs // LONG, unroll=True)
        def _(t):
            here = aligned(t, LONG)
            part = dot(
                projt[:, p * deep:(p + 1) * deep], outer[p * deep:(p + 1) * deep, here])
            part = part + (wide_bias if p == 0 else sq[:, here])
            if p < PARTS - 1:
                sq[:, here] = part
            else:
                active = jnp.maximum(part, 0.0)
                sq[:, here] = active * active
                gpre[:, here] = (pgt[:, here] * 2.0 * active).astype(BF16)

    half = pterm.shape[0] // 2
    core = lax.rem(row, 2)
    sent = len(pending)

    def proj_term(at):
        @pl.loop(0, half // TILE, unroll=True)
        def _(t):
            rows = pl.ds(pl.multiple_of(at * half + t * TILE, TILE), TILE)
            pterm[rows, :] = dot_t(outer[rows, :], gpre[...])

    low = lax.broadcasted_iota(jnp.int32, (seqs, LANES), 1) < I
    inner = {}
    cpart = CH // STEPS

    def left_part(p):
        @pl.loop(0, cpart * CH // LANES, unroll=True)
        def _(t):
            part = dot(projv[aligned(p * (cpart * CH // LANES) + t, LANES), :], gpre[...]).astype(BF16)
            for k in range(PACK):
                c = (p * (cpart // PACK) + t) * PACK + k
                for h in range(JH):
                    gouter[h * CH:(h + 1) * CH, aligned(c, LANES)] = (
                        part[k * CH:(k + 1) * CH, h * LANES:(h + 1) * LANES])

        @pl.loop(0, cpart * LANES // LONG, unroll=True)
        def _(t):
            part = dot(r2t[...], gouter[:, aligned(p * (cpart * LANES // LONG) + t, LONG)])
            done = []
            for g in range(LONG // LANES // JL):
                tiles = [
                    [
                        part[b * seqs:(b + 1) * seqs, (g * JL + k) * LANES:(g * JL + k + 1) * LANES]
                        for b in range(JL)
                    ]
                    for k in range(JL)
                ]
                done.append(fold(tiles, low, I))
            total = jnp.concatenate(done, axis=1).reshape(C, lseq, LONG // JL)
            lown[p, :, :, aligned(t, LONG // JL)] = total
            lsend[p, :, :, aligned(t, LONG // JL)] = total.astype(BF16)

    def left_send(p):
        for d in list(range(1, C1)) + [0]:
            for k in range(1, C2):
                inner[p, d, k] = go(send(
                    lsend.at[p, zpeer(d) * C2 + xpeer(k)], lxparts.at[p, k - 1, d],
                    s_lsx.at[p, k - 1, d], r_lsx.at[p, k - 1, d], row, z * C2 + xpeer(k)))

    if share:
        other = row + 1 - 2 * core
        count = half // share
        far = z // 2
        me = ((row // 2) * 2 + lax.rem(z, 2)) * C2 + x
        proj_term(1 - core)
        psend[...] = pterm[aligned(1 - core, half), :].astype(BF16)
        swap = go(send(psend, precv, s_pc, r_pc, other, col))
        proj_term(core)

        def owner(k):
            near = lax.rem(k // C2, 2)
            return (k // (2 * C2)) * 2 + core, (far * 2 + near) * C2 + lax.rem(k, C2)

        def spread_sum():
            swap.wait_recv()
            both = (pterm[aligned(core, half), :] + precv[...].astype(F32)).reshape(count, share, PAIR)
            psum[...] = both
            pshare[...] = both.astype(BF16)
            scatter = []
            for d in range(1, count):
                k = lax.rem(me + d, count)
                scatter.append(go(send(
                    pshare.at[k], pparts.at[d - 1], s_ps.at[d - 1], r_ps.at[d - 1], *owner(k))))
            return scatter

        def cross():
            for copy in scatter:
                copy.wait_recv()
            total = psum[me]
            for d in range(1, count):
                total = total + pparts[d - 1].astype(F32)
            pmid[...] = total.astype(BF16)
            return go(send(
                pmid, pcross, s_px, r_px, row, ((1 - far) * 2 + lax.rem(z, 2)) * C2 + x))

        def share_out(copy):
            copy.wait_recv()
            pgather[core, me] = (pmid[...].astype(F32) + pcross[...].astype(F32)).astype(BF16)
            for d in range(1, count):
                k = lax.rem(me + d, count)
                go(send(
                    pgather.at[core, me], pgather.at[core, me], s_pa.at[d - 1], r_pa.at[d - 1],
                    *owner(k)))
    else:
        proj_term(0)
        proj_term(1)

    left_part(0)
    left_part(1)
    if share:
        scatter = spread_sum()
    left_send(0)
    left_send(1)
    for p in range(2, STEPS):
        left_part(p)
        left_send(p)

    @pl.loop(0, JH * CH // TILE, unroll=True)
    def _(t):
        part = dot(gouter[aligned(t, TILE), :], bt[...]) * scale
        for h in range(TILE // CH):
            for a in range(JL):
                rtmp[aligned((t * (TILE // CH) + h) * JL + a, CH), :] = (
                    part[h * CH:(h + 1) * CH, a * seqs:(a + 1) * seqs])

    turned = rtmp[...].T.reshape(R, seqs // R, rwide)
    rown[...] = turned
    rsend[...] = turned.astype(BF16)
    rights = [
        go(send(rsend.at[rpeer(d)], rparts.at[d - 1], s_rs.at[d - 1], r_rs.at[d - 1], rpeer(d), col))
        for d in range(1, R)
    ]

    outers = {}

    def pass_sums(p):
        for d in range(1, C1):
            total = lown[p, zpeer(d) * C2 + x]
            for k in range(1, C2):
                inner[p, d, k].wait_recv()
                total = total + lxparts[p, k - 1, d].astype(F32)
            lzsend[p, d - 1] = total.astype(BF16)
            outers[p, d] = go(send(
                lzsend.at[p, d - 1], lzparts.at[p, d - 1], s_lsz.at[p, d - 1],
                r_lsz.at[p, d - 1], row, zpeer(d) * C2 + x))

    drain(len(pending) - sent)
    if share:
        crossed = cross()
    else:
        proj_out[...] = pterm[...]
    pass_sums(0)
    pass_sums(1)

    @pl.loop(0, JH, unroll=True)
    def _(h):
        block = sq[:, aligned(h, LANES)].T
        for a in range(JL):
            pairs_f[pl.ds(h * JL + a, I, stride=J), :] = block[a * I:(a + 1) * I, :]

    pair_out[...] = pairs_f[...].reshape(I, J, PAIR).astype(BF16)

    if share:
        share_out(crossed)
    for p in range(2, STEPS):
        pass_sums(p)

    for copy in rights:
        copy.wait_recv()
    total = rown[row]
    for d in range(1, R):
        total = total + rparts[d - 1].astype(F32)
    right_out[...] = total

    lstep = lwide // STEPS

    def left_sum(p):
        total = lown[p, col]
        for k in range(1, C2):
            inner[p, 0, k].wait_recv()
            total = total + lxparts[p, k - 1, 0].astype(F32)
        for d in range(1, C1):
            outers[p, d].wait_recv()
            total = total + lzparts[p, d - 1].astype(F32)
        lperm[p * lstep:(p + 1) * lstep, :] = total.T

    for p in range(STEPS - 1):
        left_sum(p)
    drain(3)

    if share:
        for d in range(1, count):
            k = lax.rem(me + count - d, count)
            send(
                pgather.at[core, me], pgather.at[core, k], s_pa.at[d - 1], r_pa.at[d - 1],
                *owner(k)).wait_recv()
        swap = go(send(pgather.at[core], pgather.at[core], s_pe, r_pe, other, col))

    left_sum(STEPS - 1)
    for g in range(lwide // LANES):
        block = jnp.concatenate(
            [lperm[pl.ds(g * PACK + a, CH, stride=I), :] for a in range(PACK)], axis=0)
        left_out[:, g * LANES:(g + 1) * LANES] = block.T

    if share:
        send(pgather.at[core], pgather.at[1 - core], s_pe, r_pe, other, col).wait_recv()
        proj_out[...] = pgather[...].reshape(2 * half, PAIR)

    drain()


def finish(pair, left, right, proj, pair_out, left_out, right_out, proj_out, wide, sems):
    ends = ((pair, pair_out), (left, left_out), (right, right_out), (wide, proj_out))
    stores = [pltpu.make_async_copy(src, dst, sems.at[k]) for k, (src, dst) in enumerate(ends)]
    for copy in stores[:3]:
        copy.start()
    wide[...] = proj[...].astype(F32)
    stores[3].start()
    for copy in stores:
        copy.wait()


def solution(mesh):
    R, C = mesh.shape["row"], mesh.shape["col"]

    def step(left, right, proj, bias, pair_grad):
        lseq, lwide = left.shape
        rseq, rwide = right.shape
        seqs = lseq * C
        outer_size = proj.shape[0]
        I, J = lwide // CH, rwide // CH
        JL = LANES // I
        JH = J // JL
        pairs = I * J
        C2 = inner_size(C)
        C1 = C // C2
        lchunk = lwide // PARTS
        lstep = lwide // STEPS
        half = outer_size // 2
        share = half // (R * C2) if R % 2 == 0 and C1 == 4 else 0
        if share % 16:
            share = 0
        keep = share or half
        count = half // keep
        some = max(count - 1, 1)
        dma = pltpu.SemaphoreType.DMA
        V = pltpu.VMEM
        scratch = [
            V(proj.shape, BF16), V((1, PAIR), F32), V(pair_grad.shape, BF16), V(left.shape, BF16),
            V((PARTS, C, lseq, lchunk), BF16), V((R, rseq, rwide), BF16),
            V((CH * LANES, JL * seqs), BF16), V((rwide, seqs), F32), V((JH * CH, JL * seqs), BF16),
            V((JL * seqs, JH * CH), BF16), V((PAIR, outer_size), BF16), V((pairs, PAIR), F32),
            V((PAIR, pairs), F32), V((PAIR, pairs), F32), V((outer_size, pairs), BF16),
            V((PAIR, pairs), BF16), V((JH * CH, CH * LANES), BF16), V((lwide, lseq), F32),
            V((outer_size, PAIR), F32), V((half, PAIR), BF16), V((half, PAIR), BF16),
            V((count, keep, PAIR), F32), V((count, keep, PAIR), BF16),
            V((some, keep, PAIR), BF16), V((keep, PAIR), BF16), V((keep, PAIR), BF16),
            V((2, count, keep, PAIR), BF16),
            V((rwide, seqs), F32), V((R, rseq, rwide), F32), V((R, rseq, rwide), BF16),
            V((R - 1, rseq, rwide), BF16),
            V((STEPS, C, lseq, lstep), F32), V((STEPS, C, lseq, lstep), BF16),
            V((STEPS, C2 - 1, C1, lseq, lstep), BF16), V((STEPS, C1 - 1, lseq, lstep), BF16),
            V((STEPS, C1 - 1, lseq, lstep), BF16),
            dma((PARTS, C1 - 1)), dma((PARTS, C1 - 1)),
            dma((PARTS, C2 - 1, C1)), dma((PARTS, C2 - 1, C1)),
            dma((R - 1,)), dma((R - 1,)),
            dma, dma, dma((some,)), dma((some,)), dma, dma, dma((some,)), dma((some,)), dma, dma,
            dma((R - 1,)), dma((R - 1,)),
            dma((STEPS, C2 - 1, C1)), dma((STEPS, C2 - 1, C1)),
            dma((STEPS, C1 - 1)), dma((STEPS, C1 - 1)),
            dma((2,)), dma((3,)),
        ]
        vmem = pl.BlockSpec(memory_space=pltpu.VMEM)
        hbm = pl.BlockSpec(memory_space=pl.ANY)
        pair_out, left_grad, right_grad, proj_grad = pl.pallas_call(
            functools.partial(kernel, R, C, share),
            out_shape=(
                V(pair_grad.shape, BF16), V(left.shape, F32), V(right.shape, F32),
                V(proj.shape, BF16 if share else F32),
            ),
            in_specs=[hbm] * 5,
            out_specs=[vmem] * 4,
            scratch_shapes=scratch,
            compiler_params=pltpu.CompilerParams(
                collective_id=0, has_side_effects=True, vmem_limit_bytes=60 << 20),
        )(left, right, proj, bias.reshape(1, -1), pair_grad)
        if not share:
            proj_grad = lax.psum(proj_grad, ("row", "col"))
        return pl.pallas_call(
            finish,
            out_shape=(
                jax.ShapeDtypeStruct(pair_grad.shape, BF16),
                jax.ShapeDtypeStruct(left.shape, F32),
                jax.ShapeDtypeStruct(right.shape, F32),
                jax.ShapeDtypeStruct(proj.shape, F32),
            ),
            in_specs=[vmem] * 4,
            out_specs=[hbm] * 4,
            scratch_shapes=[V(proj.shape, F32), dma((4,))],
        )(*(
            pltpu.with_memory_space_constraint(part, pltpu.VMEM)
            for part in (pair_out, left_grad, right_grad, proj_grad)
        ))

    return jax.shard_map(
        step,
        mesh=mesh,
        in_specs=(P("col", "row"), P("row", "col"), P(), P(), P("row", "col", None)),
        out_specs=(P("row", "col", None), P("col", "row"), P("row", "col"), P()),
        check_vma=False,
    )
```
